32 devices in a mesh: row: 8 (over y, x, core), col: 4 (over z).
Axes of the slice: x: 2, y: 2, z: 4, core: 2. Of those that a mesh axis runs over, the one named last changes fastest.
Arguments:
- amplitudes: bfloat16 [24576, 24576], P('col', 'row'), may hold values from -0.0390625 to 0.0390625
- cholesky: bfloat16 [24576, 1280], P(('row', 'col')), may hold values from -5 to 5
- occ_map: int32 [24576], replicated, may hold values from 0 to 47
- vir_map: int32 [24576], replicated, may hold values from 0 to 511
Outputs:
- new_amplitudes: bfloat16 [24576, 24576], P('col', 'row')
The draws below stay inside these ranges and needn't reach their ends.
All inputs are finite; a program needn't handle non-finite values.
Results may differ from the reference program's by a relative error of at most 0.0056.
Values may be sent and summed in bfloat16 or wider, within the bound.
No kernel may reach another device: no remote copies, remote signals or barrier semaphores. Data moves between devices by JAX's collectives and lax.ppermute only.
A program may use at most 192 MiB of HBM per device.

```python
import jax
import jax.numpy as jnp
from jax import lax

M = 24576
NAUX = 1280
NOCC = 48
NVIR = 512


def place_ends(values, own_key, least, largest):
    dims = values.shape
    index_at = [jax.random.randint(jax.random.fold_in(own_key, axis), (), 0, dims[axis]) for axis in range(len(dims))]
    values = values.at[tuple(index_at)].set(least)
    longest = dims.index(max(dims))
    index_at[longest] = (index_at[longest] + 1) % dims[longest]
    return values.at[tuple(index_at)].set(largest)


def levels(rng, dims, split, smallest, largest):
    factor_of = 1.0
    for position, blocks in split:
        heights = jax.random.uniform(jax.random.fold_in(jax.random.fold_in(rng, 6), position), (blocks,), jnp.float32, smallest / len(split), largest / len(split))
        factor_of = factor_of * jnp.repeat(jnp.exp(heights), dims[position] // blocks).reshape((-1,) + (1,) * (len(dims) - 1 - position))
    return factor_of


def centred(stream_key, dims, scale, most, shards=(), dtype=jnp.bfloat16):
    array = jax.random.normal(stream_key, dims, jnp.float32) * scale
    if len(shards) > 0:
        array = levels(stream_key, dims, shards, -0.22, 0.18) * array
    return jnp.clip(array, min=-most, max=most).astype(dtype)


def setup_inputs(seed: int = 0) -> dict:
    seeds = jax.random.split(jax.random.key(seed), 5)
    return {
        "amplitudes": centred(seeds[0], (M, M), M ** -0.5, 0.0390625, ((0, 4), (1, 8))),
        "cholesky": centred(seeds[1], (M, NAUX), 0.35, 5.0, ((0, 32),)),
        "occ_map": place_ends(jax.random.randint(seeds[2], (M,), 0, NOCC), jax.random.fold_in(seeds[2], 1), 0, NOCC - 1).astype(jnp.int32),
        "vir_map": place_ends(jax.random.randint(seeds[3], (M,), 0, NVIR), jax.random.fold_in(seeds[3], 1), 0, NVIR - 1).astype(jnp.int32),
    }


def pair_gap(occ_map, vir_map):
    occ = occ_map.astype(jnp.float32)
    vir = vir_map.astype(jnp.float32)
    return 0.5 + 2.5 * jnp.sqrt(vir / NVIR) + (0.5 + 2.5 * occ / NOCC)

def reference(amplitudes, cholesky, occ_map, vir_map):
    dressed = (cholesky.astype(jnp.float32) + jnp.dot(amplitudes, cholesky, preferred_element_type=jnp.float32)).astype(jnp.bfloat16)
    gap = pair_gap(occ_map, vir_map)

    def one_block(args):
        rows, gap_rows = args
        cycle = lax.dot_general(rows, dressed, (((1,), (1,)), ((), ())), preferred_element_type=jnp.float32)
        return (-cycle / (gap_rows[:, None] + gap[None, :])).astype(jnp.bfloat16)
    blocks = lax.map(one_block, (dressed.reshape(8, M // 8, NAUX), gap.reshape(8, M // 8)))
    return blocks.reshape(M, M)
```

```python
import functools

import jax
import jax.numpy as jnp
from jax import lax
from jax.experimental import pallas as pl
from jax.experimental.pallas import tpu as pltpu
from jax.sharding import PartitionSpec as P

NOCC = 48
NVIR = 512
WIDE = 256
BF = jnp.bfloat16
F32 = jnp.float32


def pair_gap(occ_map, vir_map):
    occ = occ_map.astype(jnp.float32)
    vir = vir_map.astype(jnp.float32)
    return 0.5 + 2.5 * jnp.sqrt(vir / NVIR) + (0.5 + 2.5 * occ / NOCC)


def first_kernel(tile, spots, t_ref, *refs):
    count = len(refs) - 2
    out_ref, held = refs[count], refs[count + 1]
    height = refs[0].shape[0]
    step = pl.program_id(0)

    @pl.when(step == 0)
    def _():
        for n in range(count):
            held[pl.ds(pl.multiple_of(spots[n], 32), height), :] = refs[n][...]

    total = jnp.dot(t_ref[...], held[...], preferred_element_type=jnp.float32)
    if out_ref.dtype == jnp.float32:
        tall = out_ref.shape[0]
        start = pl.multiple_of(tile[pl.num_programs(0) + step], 32)
        own = held[pl.ds(start, tall), :].astype(jnp.float32)
        keep = spots[count] > 0
        total = total + jnp.where(keep, own, jnp.zeros_like(own))
    out_ref[...] = total.astype(out_ref.dtype)


def first_product(amplitudes, pieces, tile, spots, tall, steps, dtype):
    depth = amplitudes.shape[1]
    wide = pieces[0].shape[1]
    grid_spec = pltpu.PrefetchScalarGridSpec(
        num_scalar_prefetch=2,
        grid=(steps,),
        in_specs=[pl.BlockSpec((tall, depth), lambda i, a, b: (a[i], 0))]
        + [pl.BlockSpec(x.shape, lambda i, a, b: (0, 0)) for x in pieces],
        out_specs=pl.BlockSpec((tall, wide), lambda i, a, b: (i, 0)),
        scratch_shapes=[pltpu.VMEM((depth, wide), BF)],
    )
    return pl.pallas_call(
        first_kernel,
        out_shape=jax.ShapeDtypeStruct((steps * tall, wide), dtype),
        grid_spec=grid_spec,
        cost_estimate=pl.CostEstimate(
            flops=2 * steps * tall * depth * wide,
            bytes_accessed=2 * steps * tall * depth + 4 * steps * tall * wide,
            transcendentals=0,
        ),
        name="first",
    )(tile, spots, amplitudes, *pieces)


def second_kernel(groups, strips, aliased, rows_at, cols_at, *refs):
    lhs = refs[:groups]
    rhs = refs[groups : groups + strips]
    gap_rows, gap_cols = refs[groups + strips], refs[groups + strips + 1]
    out_ref = refs[-1]
    dims = (((1,), (1,)), ((), ()))

    def finish(right):
        start = 0
        total = None
        for left in lhs:
            width = left.shape[1]
            term = lax.dot_general(
                left[...], right[:, start : start + width], dims, preferred_element_type=jnp.float32
            )
            total = term if total is None else total + term
            start += width
        out_ref[...] = (-total / (gap_rows[...] + gap_cols[...])).astype(out_ref.dtype)

    if strips == 1:
        finish(rhs[0])
    else:
        for n in range(strips):

            @pl.when(pl.program_id(1) == n)
            def _(n=n):
                finish(rhs[n])


def second_product(lhs, rhs, gap_rows, gap_cols, rows_at, cols_at, tall, out, shape):
    rows = lhs[0].shape[0]
    steps, strips = rows // tall, len(rhs)
    width, naux = rhs[0].shape
    in_specs = [pl.BlockSpec((tall, x.shape[1]), lambda i, d, a, b: (i, 0)) for x in lhs]
    in_specs += [pl.BlockSpec(x.shape, lambda i, d, a, b: (0, 0)) for x in rhs]
    in_specs += [
        pl.BlockSpec((tall, 1), lambda i, d, a, b: (a[i], 0)),
        pl.BlockSpec((1, width), lambda i, d, a, b: (0, b[d])),
    ]
    operands = [*lhs, *rhs, gap_rows, gap_cols]
    aliases = {}
    if out is not None:
        in_specs.append(pl.BlockSpec(memory_space=pl.ANY))
        aliases = {2 + len(operands): 0}
        operands.append(out)
    grid_spec = pltpu.PrefetchScalarGridSpec(
        num_scalar_prefetch=2,
        grid=(steps, strips),
        in_specs=in_specs,
        out_specs=pl.BlockSpec((tall, width), lambda i, d, a, b: (a[i], b[d])),
    )
    return pl.pallas_call(
        functools.partial(second_kernel, len(lhs), strips, out is not None),
        out_shape=jax.ShapeDtypeStruct(shape, BF),
        grid_spec=grid_spec,
        input_output_aliases=aliases,
        cost_estimate=pl.CostEstimate(
            flops=2 * rows * strips * width * naux,
            bytes_accessed=2 * rows * (naux + strips * width),
            transcendentals=0,
        ),
        name="second",
    )(rows_at, cols_at, *operands)


def body(layers, amplitudes, cholesky, occ_map, vir_map):
    tile_rows, tile_cols = amplitudes.shape
    piece, naux = cholesky.shape
    wide = WIDE if naux % WIDE == 0 else naux
    chunks = naux // wide
    row = lax.axis_index("row")
    c = lax.axis_index("col")
    k, j = row // 2, row % 2
    half = tile_rows // 2
    mid = piece // 2

    def ring(x, y):
        up = [(n, (n + 1) % layers) for n in range(layers)]
        down = [(n, (n - 1) % layers) for n in range(layers)]
        tops, bots = [x], [y]
        for _ in range(layers - 1):
            tops.append(lax.ppermute(tops[-1], "col", up))
            bots.append(lax.ppermute(bots[-1], "col", down))
        return tops, bots

    def across(x, d):
        return lax.ppermute(x, "row", [(n, n ^ (2 * d)) for n in range(2 * layers)])

    def swap(x):
        return lax.ppermute(x, "row", [(n, n ^ 1) for n in range(2 * layers)])

    order = jnp.arange(layers, dtype=jnp.int32)
    chips = jnp.bitwise_xor(k, order)
    tile_keep = jnp.concatenate([j * layers + chips, chips * piece]).astype(jnp.int32)
    tile_send = ((1 - j) * layers + chips).astype(jnp.int32)
    spots = jnp.concatenate(
        [
            ((c - order) % layers) * piece,
            ((c + order) % layers) * piece + mid,
            (k == c).astype(jnp.int32)[None],
        ]
    ).astype(jnp.int32)

    shares = []
    for n in range(chunks):
        x = cholesky[:, n * wide : (n + 1) * wide]
        tops, bots = ring(x[:mid], x[mid:])
        pieces = tops + bots
        sent = first_product(amplitudes, pieces, jnp.concatenate([tile_send, tile_send]), spots, piece, layers, BF)
        kept = first_product(amplitudes, pieces, tile_keep, spots, piece, layers, F32)
        came = swap(sent)
        both = lambda d: kept[d * piece : (d + 1) * piece] + came[d * piece : (d + 1) * piece].astype(F32)
        total = both(0)
        for d in range(1, layers):
            total = total + across(both(d).astype(BF), d).astype(F32)
        shares.append(total.astype(BF))

    splits = [(0, chunks // 2 + 1), (chunks // 2 + 1, chunks)] if chunks > 2 else [(0, chunks)]
    near, far = [], []
    for lo, hi in splits:
        mine = jnp.concatenate(shares[lo:hi], axis=1)
        if layers == 4:
            a, b = across(mine, 1), across(mine, 2)
            e, f = across(a[:mid], 2), across(b[mid:], 1)
            parts = [mine, a, b, e, f]
        else:
            parts = [mine] + [across(mine, d) for d in range(1, layers)]
        near.append(jnp.concatenate(parts, axis=0))
        far.append(swap(near[-1]))

    strips = 3 if piece % (3 * 128) == 0 else 1
    aligned = piece % (strips * 128) == 0
    width = piece // strips
    gap_rows = pair_gap(
        lax.dynamic_slice_in_dim(occ_map, c * tile_rows, tile_rows, 0),
        lax.dynamic_slice_in_dim(vir_map, c * tile_rows, tile_rows, 0),
    )[:, None]
    gap_cols = pair_gap(
        lax.dynamic_slice_in_dim(occ_map, row * tile_cols, tile_cols, 0),
        lax.dynamic_slice_in_dim(vir_map, row * tile_cols, tile_cols, 0),
    )[None, :]
    rows_near = (j * layers + chips).astype(jnp.int32)
    rows_far = ((1 - j) * layers + chips).astype(jnp.int32)
    out = None
    for s in range(strips):
        lo, cut = s * width, s * width + width // 2
        hi = lo + width
        if s == 0:
            rings = [ring(x[lo:cut], x[cut:hi]) for x in shares]
            tops = [jnp.concatenate([r[0][n] for r in rings], axis=1) for n in range(layers)]
            bots = [jnp.concatenate([r[1][n] for r in rings], axis=1) for n in range(layers)]
        else:
            tops, bots = ring(
                jnp.concatenate([x[lo:cut] for x in shares], axis=1),
                jnp.concatenate([x[cut:hi] for x in shares], axis=1),
            )
        rhs = []
        for d in range(layers):
            owner = jnp.bitwise_xor(k, d)
            block = jnp.concatenate(
                [
                    lax.select_n((c - owner) % layers, *tops) if layers != 2 else jnp.where(c == owner, tops[0], tops[1]),
                    lax.select_n((owner - c) % layers, *bots) if layers != 2 else jnp.where(c == owner, bots[0], bots[1]),
                ],
                axis=0,
            )
            rhs.append(block if d == 0 else across(block, d))
        if aligned:
            cols_at = (chips * strips + s).astype(jnp.int32)
        else:
            whole = jnp.zeros((tile_cols, naux), BF)
            for d in range(layers):
                whole = lax.dynamic_update_slice_in_dim(whole, rhs[d], chips[d] * piece, 0)
            rhs = [whole]
            cols_at = jnp.zeros((1,), jnp.int32)
        shape = (tile_rows, tile_cols)
        out = second_product(near, rhs, gap_rows, gap_cols, rows_near, cols_at, piece, out, shape)
        out = second_product(far, rhs, gap_rows, gap_cols, rows_far, cols_at, piece, out, shape)
    return out


def solution(mesh):
    layers = mesh.shape["col"]
    assert mesh.shape["row"] == 2 * layers
    return jax.shard_map(
        functools.partial(body, layers),
        mesh=mesh,
        in_specs=(P("col", "row"), P(("row", "col"), None), P(), P()),
        out_specs=P("col", "row"),
        check_vma=False,
    )
```

```python
import functools

import jax
import jax.numpy as jnp
from jax import lax
from jax.experimental import pallas as pl
from jax.experimental.pallas import tpu as pltpu
from jax.sharding import PartitionSpec as P

NOCC = 48
NVIR = 512
LANES = 128
BF = jnp.bfloat16
F32 = jnp.float32


def pair_gap(occ_map, vir_map):
    occ = occ_map.astype(jnp.float32)
    vir = vir_map.astype(jnp.float32)
    return 0.5 + 2.5 * jnp.sqrt(vir / NVIR) + (0.5 + 2.5 * occ / NOCC)


def first_kernel(keep, spots, chips, t_ref, *refs):
    count = len(refs) - 2
    out_ref, held = refs[count], refs[count + 1]
    height = refs[0].shape[0]
    width = out_ref.shape[2]
    step, phase = pl.program_id(0), pl.program_id(1)
    count_in = t_ref.shape[0] // width

    @pl.when(jnp.logical_and(step == 0, phase == 0))
    def _():
        for n in range(count):

            @pl.when(spots[n] >= 0)
            def _(n=n):
                held[pl.ds(pl.multiple_of(spots[n], 32), height), :] = refs[n][...]

    total = jnp.dot(t_ref[...], held[...], preferred_element_type=jnp.float32)
    if keep:
        tall = count_in * width
        at = (step * pl.num_programs(1) + phase) * tall
        own = held[pl.ds(pl.multiple_of(at, 32), tall), :].astype(jnp.float32)
        total = total + jnp.where(spots[count] > 0, own, jnp.zeros_like(own))
    for n in range(count_in):
        out_ref[chips[phase * count_in + n], 0] = total[n * width : (n + 1) * width]


def first_product(amplitudes, pieces, spots, chips, layers, strips, keep):
    tile_rows, depth = amplitudes.shape
    wide = pieces[0].shape[1]
    tall = tile_rows // (2 * strips)
    width = tall // layers
    grid_spec = pltpu.PrefetchScalarGridSpec(
        num_scalar_prefetch=2,
        grid=(strips, 2),
        in_specs=[
            pl.BlockSpec((tall // 2, depth), lambda i, h, a, b: ((b[layers + 1 - int(keep)] * strips + i) * 2 + h, 0))
        ]
        + [pl.BlockSpec(x.shape, lambda i, h, a, b: (0, 0)) for x in pieces],
        out_specs=pl.BlockSpec((layers, 1, width, wide), lambda i, h, a, b: (0, i, 0, 0)),
        scratch_shapes=[pltpu.VMEM((depth, wide), BF)],
    )
    out = pl.pallas_call(
        functools.partial(first_kernel, keep),
        out_shape=jax.ShapeDtypeStruct((layers, strips, width, wide), F32),
        grid_spec=grid_spec,
        cost_estimate=pl.CostEstimate(
            flops=tile_rows * depth * wide,
            bytes_accessed=tile_rows * depth + 2 * tile_rows * wide,
            transcendentals=0,
        ),
        name="first",
    )(spots, chips, amplitudes, *pieces)
    return out.reshape(layers * strips * width, wide)


def second_kernel(groups, layers, place, chips, *refs):
    lhs = refs[:groups]
    rhs = refs[groups : groups + layers]
    gap_rows, gap_cols = refs[groups + layers], refs[groups + layers + 1]
    out_ref, left, right = refs[-3], refs[-2], refs[-1]
    dims = (((1,), (1,)), ((), ()))
    width = rhs[0].shape[0]

    @pl.when(pl.program_id(0) == 0)
    def _():
        for n in range(layers):
            right[pl.ds(pl.multiple_of(chips[n] * width, 32), width), :] = rhs[n][...]

    start = 0
    for part in lhs:
        wide = part.shape[3]
        for n in range(layers):
            left[n * width : (n + 1) * width, start : start + wide] = part[chips[n], 0]
        start += wide
    broad = out_ref.shape[1]
    pick = 512 if broad % 512 == 0 else broad
    rows = jnp.transpose(jnp.broadcast_to(gap_rows[...], (LANES, gap_rows.shape[1])))[:, :1]
    for n in range(0, broad, pick):
        total = lax.dot_general(
            left[...], right[n : n + pick, :], dims, preferred_element_type=jnp.float32
        )
        out_ref[:, n : n + pick] = (-total / (rows + gap_cols[:, n : n + pick])).astype(out_ref.dtype)


def second_product(lhs, rhs, gap_rows, gap_cols, place, chips, strips, out, shape):
    layers = len(rhs)
    width, naux = rhs[0].shape
    tall = layers * width
    lhs = [x.reshape(layers, strips, width, x.shape[1]) for x in lhs]
    in_specs = [pl.BlockSpec((layers, 1, width, x.shape[3]), lambda i, a, b: (0, i, 0, 0)) for x in lhs]
    in_specs += [pl.BlockSpec((width, naux), lambda i, a, b: (0, 0)) for x in rhs]
    in_specs += [
        pl.BlockSpec((1, tall), lambda i, a, b: (0, a[0] * strips + i)),
        pl.BlockSpec((1, tall), lambda i, a, b: (0, a[1])),
    ]
    operands = [*lhs, *rhs, gap_rows, gap_cols]
    aliases = {}
    if out is not None:
        in_specs.append(pl.BlockSpec(memory_space=pl.ANY))
        aliases = {2 + len(operands): 0}
        operands.append(out)
    grid_spec = pltpu.PrefetchScalarGridSpec(
        num_scalar_prefetch=2,
        grid=(strips,),
        in_specs=in_specs,
        out_specs=pl.BlockSpec((tall, tall), lambda i, a, b: (a[0] * strips + i, a[1])),
        scratch_shapes=[pltpu.VMEM((tall, naux), BF), pltpu.VMEM((tall, naux), BF)],
    )
    return pl.pallas_call(
        functools.partial(second_kernel, len(lhs), layers),
        out_shape=jax.ShapeDtypeStruct(shape, BF),
        grid_spec=grid_spec,
        input_output_aliases=aliases,
        cost_estimate=pl.CostEstimate(
            flops=2 * strips * tall * tall * naux,
            bytes_accessed=2 * strips * tall * (naux + tall),
            transcendentals=0,
        ),
        name="second",
    )(place, chips, *operands)


def body(layers, amplitudes, cholesky, occ_map, vir_map):
    tile_rows, tile_cols = amplitudes.shape
    piece, naux = cholesky.shape
    row = lax.axis_index("row")
    c = lax.axis_index("col")
    k, j = row // 2, row % 2
    mid = piece // 2
    strips = 3 if piece % 768 == 0 else 1
    width = piece // strips
    cut = (2 * naux // 5) // 256 * 256
    spans = [(0, cut), (cut, naux)] if cut else [(0, naux)]
    chunks = len(spans)

    def line(x):
        ups, downs = [x], [x]
        for s in range(1, layers):
            up = [(n, n + 1) for n in range(s - 1, layers - 1)]
            down = [(layers - 1 - a, layers - 1 - b) for a, b in up]
            ups.append(lax.ppermute(ups[-1], "col", up))
            downs.append(lax.ppermute(downs[-1], "col", down))
        return ups[:0:-1] + [x] + downs[1:]

    def across(x, d):
        return lax.ppermute(x, "row", [(n, n ^ (2 * d)) for n in range(2 * layers)])

    def swap(x):
        return lax.ppermute(x, "row", [(n, n ^ 1) for n in range(2 * layers)])

    reach = jnp.arange(1 - layers, layers, dtype=jnp.int32) + c
    chips = jnp.bitwise_xor(k, jnp.arange(layers, dtype=jnp.int32))
    sides = jnp.concatenate([chips, jnp.stack([j, 1 - j])]).astype(jnp.int32)
    spots = jnp.where(jnp.logical_and(reach >= 0, reach < layers), reach * piece, -1)
    spots = jnp.concatenate([spots, (k == c).astype(jnp.int32)[None]]).astype(jnp.int32)

    gap_rows = pair_gap(
        lax.dynamic_slice_in_dim(occ_map, c * tile_rows, tile_rows, 0),
        lax.dynamic_slice_in_dim(vir_map, c * tile_rows, tile_rows, 0),
    )[None, :]
    gap_cols = pair_gap(
        lax.dynamic_slice_in_dim(occ_map, row * tile_cols, tile_cols, 0),
        lax.dynamic_slice_in_dim(vir_map, row * tile_cols, tile_cols, 0),
    )[None, :]

    shares = []
    for lo, hi in spans:
        pieces = line(cholesky[:, lo:hi])
        sent = first_product(amplitudes, pieces, spots, sides, layers, strips, False)
        kept = first_product(amplitudes, pieces, spots, sides, layers, strips, True)
        came = swap(sent)

        def both(d, part=None, kept=kept, came=came):
            at = slice(d * piece, (d + 1) * piece)
            if part is not None:
                at = slice(d * piece + part * mid, d * piece + (part + 1) * mid)
            return kept[at] + came[at]

        if layers == 4:
            a0 = jnp.concatenate([both(1, 0), both(3, 0)]).astype(BF)
            b0 = jnp.concatenate([both(2, 1), both(3, 1)]).astype(BF)
            a1, b1 = across(a0, 1), across(b0, 2)
            kept, came, a1, b1 = lax.optimization_barrier((kept, came, a1, b1))
            a2 = (both(2, 0, kept, came) + a1[mid:].astype(F32)).astype(BF)
            b2 = (both(1, 1, kept, came) + b1[mid:].astype(F32)).astype(BF)
            a2, b2 = across(a2, 2), across(b2, 1)
            kept, came, a1, b1, a2, b2 = lax.optimization_barrier((kept, came, a1, b1, a2, b2))
            top = both(0, 0, kept, came) + a1[:mid].astype(F32) + a2.astype(F32)
            low = both(0, 1, kept, came) + b1[:mid].astype(F32) + b2.astype(F32)
            total = jnp.concatenate([top, low])
        else:
            total = both(0)
            for d in range(1, layers):
                total = total + across(both(d).astype(BF), d).astype(F32)
        shares.append(total.astype(BF))

    splits = [(0, chunks - 1), (chunks - 1, chunks)] if chunks > 1 else [(0, 1)]
    near, far = [], []
    for lo, hi in splits:
        mine = jnp.concatenate(shares[lo:hi], axis=1)
        if layers == 4:
            a, b = across(mine, 1), across(mine, 2)
            parts = [mine, a, b, across(a[:mid], 2), across(b[mid:], 1)]
        else:
            parts = [mine] + [across(mine, d) for d in range(1, layers)]
        near.append(jnp.concatenate(parts, axis=0))
        far.append(swap(near[-1]))

    early = [line(x) for x in shares[:-1]]
    near_at = lambda s: jnp.stack([j, jnp.full_like(j, s)]).astype(jnp.int32)
    far_at = lambda s: jnp.stack([1 - j, jnp.full_like(j, s)]).astype(jnp.int32)
    out = None
    for s in range(strips):
        at = slice(s * width, (s + 1) * width)
        late = line(shares[-1][at])
        ahead, late = lax.optimization_barrier((early, late))
        rows = [[x[at] for x in group] for group in ahead] + [late]

        def block(d, rows=rows):
            owner = jnp.bitwise_xor(k, d) - c + layers - 1
            return jnp.concatenate([lax.select_n(owner, *group) for group in rows], axis=1)

        blocks = [block(d) for d in range(layers)]
        pair = jnp.concatenate([blocks[1], blocks[-1]])
        if layers == 4:
            one = across(pair, 1)
            two = across(blocks[2], 2)
            rest = one[width:]
            rhs = [blocks[0], one, two, across(rest, 2)]
        else:
            rhs = [blocks[0]] + [across(blocks[d], d) for d in range(1, layers)]
        shape = (tile_rows, tile_cols)
        out = second_product(near, rhs, gap_rows, gap_cols, near_at(s), sides, strips, out, shape)
        out = second_product(far, rhs, gap_rows, gap_cols, far_at(s), sides, strips, out, shape)
    return out


def solution(mesh):
    layers = mesh.shape["col"]
    assert mesh.shape["row"] == 2 * layers

    def run(*args):
        return body(layers, *args)

    return jax.shard_map(
        run,
        mesh=mesh,
        in_specs=(P("col", "row"), P(("row", "col"), None), P(), P()),
        out_specs=P("col", "row"),
        check_vma=False,
    )
```

```python
import functools

import jax
import jax.numpy as jnp
from jax import lax
from jax.experimental import pallas as pl
from jax.experimental.pallas import tpu as pltpu
from jax.sharding import PartitionSpec as P

NOCC = 48
NVIR = 512
LANES = 128
BF = jnp.bfloat16
F32 = jnp.float32


def pair_gap(occ_map, vir_map):
    occ = occ_map.astype(jnp.float32)
    vir = vir_map.astype(jnp.float32)
    return 0.5 + 2.5 * jnp.sqrt(vir / NVIR) + (0.5 + 2.5 * occ / NOCC)


def first_kernel(keep, spots, chips, t_ref, *refs):
    count = len(refs) - 2
    out_ref, held = refs[count], refs[count + 1]
    height = refs[0].shape[0]
    width = out_ref.shape[2]
    step, phase = pl.program_id(0), pl.program_id(1)
    count_in = t_ref.shape[0] // width

    @pl.when(jnp.logical_and(step == 0, phase == 0))
    def _():
        for n in range(count):

            @pl.when(spots[n] >= 0)
            def _(n=n):
                held[pl.ds(pl.multiple_of(spots[n], 32), height), :] = refs[n][...]

    total = jnp.dot(t_ref[...], held[...], preferred_element_type=jnp.float32)
    if keep:
        tall = count_in * width
        at = (step * pl.num_programs(1) + phase) * tall
        own = held[pl.ds(pl.multiple_of(at, 32), tall), :].astype(jnp.float32)
        total = total + jnp.where(spots[count] > 0, own, jnp.zeros_like(own))
    for n in range(count_in):
        out_ref[chips[phase * count_in + n], 0] = total[n * width : (n + 1) * width]


def first_product(amplitudes, pieces, spots, chips, layers, strips, keep):
    tile_rows, depth = amplitudes.shape
    wide = pieces[0].shape[1]
    tall = tile_rows // (2 * strips)
    width = tall // layers
    grid_spec = pltpu.PrefetchScalarGridSpec(
        num_scalar_prefetch=2,
        grid=(strips, 2),
        in_specs=[
            pl.BlockSpec((tall // 2, depth), lambda i, h, a, b: ((b[layers + 1 - int(keep)] * strips + i) * 2 + h, 0))
        ]
        + [pl.BlockSpec(x.shape, lambda i, h, a, b: (0, 0)) for x in pieces],
        out_specs=pl.BlockSpec((layers, 1, width, wide), lambda i, h, a, b: (0, i, 0, 0)),
        scratch_shapes=[pltpu.VMEM((depth, wide), BF)],
    )
    out = pl.pallas_call(
        functools.partial(first_kernel, keep),
        out_shape=jax.ShapeDtypeStruct((layers, strips, width, wide), F32),
        grid_spec=grid_spec,
        cost_estimate=pl.CostEstimate(
            flops=tile_rows * depth * wide,
            bytes_accessed=tile_rows * depth + 2 * tile_rows * wide,
            transcendentals=0,
        ),
        name="first",
    )(spots, chips, amplitudes, *pieces)
    return out.reshape(layers * strips * width, wide)


def second_kernel(groups, parts, layers, place, chips, *refs):
    lhs = refs[:groups]
    rhs = refs[groups : groups + len(parts)]
    gap_rows, gap_cols = refs[groups + len(parts)], refs[groups + len(parts) + 1]
    out_ref, left, right = refs[-3], refs[-2], refs[-1]
    dims = (((1,), (1,)), ((), ()))
    width = rhs[0].shape[0]

    @pl.when(pl.program_id(0) == 0)
    def _():
        for ref, (n, lo) in zip(rhs, parts):
            right[pl.ds(pl.multiple_of(chips[n] * width + lo, 32), ref.shape[0]), :] = ref[...]

    start = 0
    for part in lhs:
        wide = part.shape[3]
        for n in range(layers):
            left[n * width : (n + 1) * width, start : start + wide] = part[chips[n], 0]
        start += wide
    broad = out_ref.shape[1]
    pick = 512 if broad % 512 == 0 else broad
    rows = jnp.transpose(jnp.broadcast_to(gap_rows[...], (LANES, gap_rows.shape[1])))[:, :1]
    for n in range(0, broad, pick):
        total = lax.dot_general(
            left[...], right[n : n + pick, :], dims, preferred_element_type=jnp.float32
        )
        out_ref[:, n : n + pick] = (-total / (rows + gap_cols[:, n : n + pick])).astype(out_ref.dtype)


def second_product(lhs, rhs, gap_rows, gap_cols, place, chips, strips, layers, out, shape):
    parts = [(n, lo) for _, n, lo in rhs]
    rhs = [x for x, _, _ in rhs]
    width, naux = rhs[0].shape
    tall = layers * width
    lhs = [x.reshape(layers, strips, width, x.shape[1]) for x in lhs]
    in_specs = [pl.BlockSpec((layers, 1, width, x.shape[3]), lambda i, a, b: (0, i, 0, 0)) for x in lhs]
    in_specs += [pl.BlockSpec((min(width, x.shape[0]), naux), lambda i, a, b: (0, 0)) for x in rhs]
    in_specs += [
        pl.BlockSpec((1, tall), lambda i, a, b: (0, a[0] * strips + i)),
        pl.BlockSpec((1, tall), lambda i, a, b: (0, a[1])),
    ]
    operands = [*lhs, *rhs, gap_rows, gap_cols]
    aliases = {}
    if out is not None:
        in_specs.append(pl.BlockSpec(memory_space=pl.ANY))
        aliases = {2 + len(operands): 0}
        operands.append(out)
    grid_spec = pltpu.PrefetchScalarGridSpec(
        num_scalar_prefetch=2,
        grid=(strips,),
        in_specs=in_specs,
        out_specs=pl.BlockSpec((tall, tall), lambda i, a, b: (a[0] * strips + i, a[1])),
        scratch_shapes=[pltpu.VMEM((tall, naux), BF), pltpu.VMEM((tall, naux), BF)],
    )
    return pl.pallas_call(
        functools.partial(second_kernel, len(lhs), parts, layers),
        out_shape=jax.ShapeDtypeStruct(shape, BF),
        grid_spec=grid_spec,
        input_output_aliases=aliases,
        cost_estimate=pl.CostEstimate(
            flops=2 * strips * tall * tall * naux,
            bytes_accessed=2 * strips * tall * (naux + tall),
            transcendentals=0,
        ),
        name="second",
    )(place, chips, *operands)


def choose_kernel(count, start, owners, *refs):
    early, late = refs[:count], refs[count : 2 * count]
    first, second, own, sems = refs[2 * count :]
    width, wide = own.shape[0], early[0].shape[1]
    cut = width // 2
    plan = [
        (0, 0, width, own, 0),
        (1, 0, width, first, 0),
        (2, 0, width, second, 0),
        (3, 0, cut, first, width),
        (3, cut, cut, second, width),
    ]

    def copies(n, i):
        _, lo, tall, out, at = plan[n]
        rest = late[i].shape[1]
        return (
            pltpu.make_async_copy(
                early[i].at[pl.ds(start + lo, tall), :],
                out.at[pl.ds(at, tall), pl.ds(0, wide)],
                sems.at[2 * n],
            ),
            pltpu.make_async_copy(
                late[i].at[pl.ds(lo, tall), :],
                out.at[pl.ds(at, tall), pl.ds(wide, rest)],
                sems.at[2 * n + 1],
            ),
        )

    for n in range(len(plan)):
        for i in range(count):

            @pl.when(owners[plan[n][0]] == i)
            def _(n=n, i=i):
                for copy in copies(n, i):
                    copy.start()

    for n in range(len(plan)):
        for copy in copies(n, 0):
            copy.wait()


def choose(owners, early, late, start):
    width = late[0].shape[0]
    naux = early[0].shape[1] + late[0].shape[1]
    both = width + width // 2
    any_spec = pl.BlockSpec(memory_space=pl.ANY)
    vmem_spec = pl.BlockSpec(memory_space=pltpu.VMEM)
    return pl.pallas_call(
        functools.partial(choose_kernel, len(early), start),
        out_shape=[jax.ShapeDtypeStruct((rows, naux), BF) for rows in (both, both, width)],
        in_specs=[pl.BlockSpec(memory_space=pltpu.SMEM)] + [any_spec] * (2 * len(early)),
        out_specs=[vmem_spec] * 3,
        scratch_shapes=[pltpu.SemaphoreType.DMA((10,))],
        cost_estimate=pl.CostEstimate(flops=0, bytes_accessed=16 * width * naux, transcendentals=0),
        name="choose",
    )(owners, *early, *late)


def body(layers, amplitudes, cholesky, occ_map, vir_map):
    tile_rows, tile_cols = amplitudes.shape
    piece, naux = cholesky.shape
    row = lax.axis_index("row")
    c = lax.axis_index("col")
    k, j = row // 2, row % 2
    mid = piece // 2
    strips = 3 if piece % 768 == 0 else 1
    width = piece // strips
    cut = (2 * naux // 5) // 256 * 256
    spans = [(0, cut), (cut, naux)] if cut else [(0, naux)]
    chunks = len(spans)

    def line(x):
        ups, downs = [x], [x]
        for s in range(1, layers):
            up = [(n, n + 1) for n in range(s - 1, layers - 1)]
            down = [(layers - 1 - a, layers - 1 - b) for a, b in up]
            ups.append(lax.ppermute(ups[-1], "col", up))
            downs.append(lax.ppermute(downs[-1], "col", down))
        return ups[:0:-1] + [x] + downs[1:]

    def across(x, d):
        return lax.ppermute(x, "row", [(n, n ^ (2 * d)) for n in range(2 * layers)])

    def swap(x):
        return lax.ppermute(x, "row", [(n, n ^ 1) for n in range(2 * layers)])

    reach = jnp.arange(1 - layers, layers, dtype=jnp.int32) + c
    chips = jnp.bitwise_xor(k, jnp.arange(layers, dtype=jnp.int32))
    sides = jnp.concatenate([chips, jnp.stack([j, 1 - j])]).astype(jnp.int32)
    spots = jnp.where(jnp.logical_and(reach >= 0, reach < layers), reach * piece, -1)
    spots = jnp.concatenate([spots, (k == c).astype(jnp.int32)[None]]).astype(jnp.int32)

    gap_rows = pair_gap(
        lax.dynamic_slice_in_dim(occ_map, c * tile_rows, tile_rows, 0),
        lax.dynamic_slice_in_dim(vir_map, c * tile_rows, tile_rows, 0),
    )[None, :]
    gap_cols = pair_gap(
        lax.dynamic_slice_in_dim(occ_map, row * tile_cols, tile_cols, 0),
        lax.dynamic_slice_in_dim(vir_map, row * tile_cols, tile_cols, 0),
    )[None, :]

    shares = []
    for lo, hi in spans:
        pieces = line(cholesky[:, lo:hi])
        sent = first_product(amplitudes, pieces, spots, sides, layers, strips, False)
        kept = first_product(amplitudes, pieces, spots, sides, layers, strips, True)
        came = swap(sent)

        def both(d, part=None, kept=kept, came=came):
            at = slice(d * piece, (d + 1) * piece)
            if part is not None:
                at = slice(d * piece + part * mid, d * piece + (part + 1) * mid)
            return kept[at] + came[at]

        if layers == 4:
            a0 = jnp.concatenate([both(1, 0), both(3, 0)]).astype(BF)
            b0 = jnp.concatenate([both(2, 1), both(3, 1)]).astype(BF)
            a1, b1 = across(a0, 1), across(b0, 2)
            kept, came, a1, b1 = lax.optimization_barrier((kept, came, a1, b1))
            a2 = (both(2, 0, kept, came) + a1[mid:].astype(F32)).astype(BF)
            b2 = (both(1, 1, kept, came) + b1[mid:].astype(F32)).astype(BF)
            a2, b2 = across(a2, 2), across(b2, 1)
            kept, came, a1, b1, a2, b2 = lax.optimization_barrier((kept, came, a1, b1, a2, b2))
            top = both(0, 0, kept, came) + a1[:mid].astype(F32) + a2.astype(F32)
            low = both(0, 1, kept, came) + b1[:mid].astype(F32) + b2.astype(F32)
            total = jnp.concatenate([top, low])
        else:
            total = both(0)
            for d in range(1, layers):
                total = total + across(both(d).astype(BF), d).astype(F32)
        shares.append(total.astype(BF))

    splits = [(0, chunks - 1), (chunks - 1, chunks)] if chunks > 1 else [(0, 1)]
    near, far = [], []
    for lo, hi in splits:
        mine = jnp.concatenate(shares[lo:hi], axis=1)
        if layers == 4:
            a, b = across(mine, 1), across(mine, 2)
            parts = [mine, a, b, across(a[:mid], 2), across(b[mid:], 1)]
        else:
            parts = [mine] + [across(mine, d) for d in range(1, layers)]
        near.append(jnp.concatenate(parts, axis=0))
        far.append(swap(near[-1]))

    early = [line(x) for x in shares[:-1]]
    near_at = lambda s: jnp.stack([j, jnp.full_like(j, s)]).astype(jnp.int32)
    far_at = lambda s: jnp.stack([1 - j, jnp.full_like(j, s)]).astype(jnp.int32)
    out = None
    for s in range(strips):
        at = slice(s * width, (s + 1) * width)
        late = line(shares[-1][at])
        owners = (chips - c + layers - 1).astype(jnp.int32)
        if layers == 4 and len(early) == 1:
            one, two, own = choose(owners, early[0], late, s * width)
            one, two = across(one, 1), across(two, 2)
            rest, more = one[width:], two[width:]
            rest, more = across(rest, 2), across(more, 1)
            rhs = [(own, 0, 0), (one, 1, 0), (two, 2, 0), (rest, 3, 0), (more, 3, width // 2)]
        else:
            rows = [[x[at] for x in group] for group in early] + [late]
            blocks = [
                jnp.concatenate([lax.select_n(owners[d], *group) for group in rows], axis=1) for d in range(layers)
            ]
            rhs = [(blocks[0], 0, 0)] + [(across(blocks[d], d), d, 0) for d in range(1, layers)]
        shape = (tile_rows, tile_cols)
        out = second_product(near, rhs, gap_rows, gap_cols, near_at(s), sides, strips, layers, out, shape)
        out = second_product(far, rhs, gap_rows, gap_cols, far_at(s), sides, strips, layers, out, shape)
    return out


def solution(mesh):
    layers = mesh.shape["col"]
    assert mesh.shape["row"] == 2 * layers

    def run(*args):
        return body(layers, *args)

    return jax.shard_map(
        run,
        mesh=mesh,
        in_specs=(P("col", "row"), P(("row", "col"), None), P(), P()),
        out_specs=P("col", "row"),
        check_vma=False,
    )
```

```python
import functools

import jax
import jax.numpy as jnp
from jax import lax
from jax.experimental import pallas as pl
from jax.experimental.pallas import tpu as pltpu
from jax.sharding import PartitionSpec as P

NOCC = 48
NVIR = 512
LANES = 128
BF = jnp.bfloat16
F32 = jnp.float32


def pair_gap(occ_map, vir_map):
    occ = occ_map.astype(jnp.float32)
    vir = vir_map.astype(jnp.float32)
    return 0.5 + 2.5 * jnp.sqrt(vir / NVIR) + (0.5 + 2.5 * occ / NOCC)


def first_kernel(keep, spots, chips, t_ref, *refs):
    count = len(refs) - 2
    out_ref, held = refs[count], refs[count + 1]
    height = refs[0].shape[0]
    width = out_ref.shape[2]
    step, phase = pl.program_id(0), pl.program_id(1)
    count_in = t_ref.shape[0] // width

    @pl.when(jnp.logical_and(step == 0, phase == 0))
    def _():
        for n in range(count):

            @pl.when(spots[n] >= 0)
            def _(n=n):
                held[pl.ds(pl.multiple_of(spots[n], 32), height), :] = refs[n][...]

    total = jnp.dot(t_ref[...], held[...], preferred_element_type=jnp.float32)
    if keep:
        tall = count_in * width
        at = (step * pl.num_programs(1) + phase) * tall
        own = held[pl.ds(pl.multiple_of(at, 32), tall), :].astype(jnp.float32)
        total = total + jnp.where(spots[count] > 0, own, jnp.zeros_like(own))
    for n in range(count_in):
        out_ref[chips[phase * count_in + n], 0] = total[n * width : (n + 1) * width]


def first_product(amplitudes, pieces, spots, chips, layers, strips, keep):
    tile_rows, depth = amplitudes.shape
    wide = pieces[0].shape[1]
    tall = tile_rows // (2 * strips)
    width = tall // layers
    grid_spec = pltpu.PrefetchScalarGridSpec(
        num_scalar_prefetch=2,
        grid=(strips, 2),
        in_specs=[
            pl.BlockSpec((tall // 2, depth), lambda i, h, a, b: ((b[layers + 1 - int(keep)] * strips + i) * 2 + h, 0))
        ]
        + [pl.BlockSpec(x.shape, lambda i, h, a, b: (0, 0)) for x in pieces],
        out_specs=pl.BlockSpec((layers, 1, width, wide), lambda i, h, a, b: (0, i, 0, 0)),
        scratch_shapes=[pltpu.VMEM((depth, wide), BF)],
    )
    out = pl.pallas_call(
        functools.partial(first_kernel, keep),
        out_shape=jax.ShapeDtypeStruct((layers, strips, width, wide), F32),
        grid_spec=grid_spec,
        cost_estimate=pl.CostEstimate(
            flops=tile_rows * depth * wide,
            bytes_accessed=tile_rows * depth + 2 * tile_rows * wide,
            transcendentals=0,
        ),
        name="first",
    )(spots, chips, amplitudes, *pieces)
    return out.reshape(layers * strips * width, wide)


def second_kernel(groups, parts, layers, place, chips, *refs):
    lhs = refs[:groups]
    rhs = refs[groups : groups + len(parts)]
    gap_rows, gap_cols = refs[groups + len(parts)], refs[groups + len(parts) + 1]
    out_ref, left, right = refs[-3], refs[-2], refs[-1]
    dims = (((1,), (1,)), ((), ()))
    width = rhs[0].shape[0]

    @pl.when(pl.program_id(0) == 0)
    def _():
        for ref, (n, lo) in zip(rhs, parts):
            right[pl.ds(pl.multiple_of(chips[n] * width + lo, 32), ref.shape[0]), :] = ref[...]

    start = 0
    for part in lhs:
        wide = part.shape[3]
        for n in range(layers):
            left[n * width : (n + 1) * width, start : start + wide] = part[chips[n], 0]
        start += wide
    broad = out_ref.shape[1]
    pick = 256 if broad % 256 == 0 else broad
    rows = jnp.transpose(jnp.broadcast_to(gap_rows[...], (LANES, gap_rows.shape[1])))[:, :1]
    for n in range(0, broad, pick):
        total = lax.dot_general(
            left[...], right[n : n + pick, :], dims, preferred_element_type=jnp.float32
        )
        out_ref[:, n : n + pick] = (-total * (1.0 / (rows + gap_cols[:, n : n + pick]))).astype(out_ref.dtype)


def second_product(lhs, rhs, gap_rows, gap_cols, place, chips, strips, layers, out, shape):
    parts = [(n, lo) for _, n, lo in rhs]
    rhs = [x for x, _, _ in rhs]
    width, naux = rhs[0].shape
    tall = layers * width
    lhs = [x.reshape(layers, strips, width, x.shape[1]) for x in lhs]
    in_specs = [pl.BlockSpec((layers, 1, width, x.shape[3]), lambda i, a, b: (0, i, 0, 0)) for x in lhs]
    in_specs += [pl.BlockSpec((min(width, x.shape[0]), naux), lambda i, a, b: (0, 0)) for x in rhs]
    in_specs += [
        pl.BlockSpec((1, tall), lambda i, a, b: (0, a[0] * strips + i)),
        pl.BlockSpec((1, tall), lambda i, a, b: (0, a[1])),
    ]
    operands = [*lhs, *rhs, gap_rows, gap_cols]
    aliases = {}
    if out is not None:
        in_specs.append(pl.BlockSpec(memory_space=pl.ANY))
        aliases = {2 + len(operands): 0}
        operands.append(out)
    grid_spec = pltpu.PrefetchScalarGridSpec(
        num_scalar_prefetch=2,
        grid=(strips,),
        in_specs=in_specs,
        out_specs=pl.BlockSpec((tall, tall), lambda i, a, b: (a[0] * strips + i, a[1])),
        scratch_shapes=[pltpu.VMEM((tall, naux), BF), pltpu.VMEM((tall, naux), BF)],
    )
    return pl.pallas_call(
        functools.partial(second_kernel, len(lhs), parts, layers),
        out_shape=jax.ShapeDtypeStruct(shape, BF),
        grid_spec=grid_spec,
        input_output_aliases=aliases,
        cost_estimate=pl.CostEstimate(
            flops=2 * strips * tall * tall * naux,
            bytes_accessed=2 * strips * tall * (naux + tall),
            transcendentals=0,
        ),
        name="second",
    )(place, chips, *operands)


def choose_kernel(count, start, owners, *refs):
    early, late = refs[:count], refs[count : 2 * count]
    first, second, own, sems = refs[2 * count :]
    width, wide = own.shape[0], early[0].shape[1]
    cut = width // 2
    plan = [
        (0, 0, width, own, 0),
        (1, 0, width, first, 0),
        (2, 0, width, second, 0),
        (3, 0, cut, first, width),
        (3, cut, cut, second, width),
    ]

    def copies(n, i):
        _, lo, tall, out, at = plan[n]
        rest = late[i].shape[1]
        return (
            pltpu.make_async_copy(
                early[i].at[pl.ds(start + lo, tall), :],
                out.at[pl.ds(at, tall), pl.ds(0, wide)],
                sems.at[2 * n],
            ),
            pltpu.make_async_copy(
                late[i].at[pl.ds(lo, tall), :],
                out.at[pl.ds(at, tall), pl.ds(wide, rest)],
                sems.at[2 * n + 1],
            ),
        )

    for n in range(len(plan)):
        for i in range(count):

            @pl.when(owners[plan[n][0]] == i)
            def _(n=n, i=i):
                for copy in copies(n, i):
                    copy.start()

    for n in range(len(plan)):
        for copy in copies(n, 0):
            copy.wait()


def choose(owners, early, late, start):
    width = late[0].shape[0]
    naux = early[0].shape[1] + late[0].shape[1]
    both = width + width // 2
    any_spec = pl.BlockSpec(memory_space=pl.ANY)
    vmem_spec = pl.BlockSpec(memory_space=pltpu.VMEM)
    return pl.pallas_call(
        functools.partial(choose_kernel, len(early), start),
        out_shape=[jax.ShapeDtypeStruct((rows, naux), BF) for rows in (both, both, width)],
        in_specs=[pl.BlockSpec(memory_space=pltpu.SMEM)] + [any_spec] * (2 * len(early)),
        out_specs=[vmem_spec] * 3,
        scratch_shapes=[pltpu.SemaphoreType.DMA((10,))],
        cost_estimate=pl.CostEstimate(flops=0, bytes_accessed=16 * width * naux, transcendentals=0),
        name="choose",
    )(owners, *early, *late)


def body(layers, amplitudes, cholesky, occ_map, vir_map):
    tile_rows, tile_cols = amplitudes.shape
    piece, naux = cholesky.shape
    row = lax.axis_index("row")
    c = lax.axis_index("col")
    k, j = row // 2, row % 2
    mid = piece // 2
    strips = 3 if piece % 768 == 0 else 1
    width = piece // strips
    cut = (2 * naux // 5) // 256 * 256
    spans = [(0, cut), (cut, naux)] if cut else [(0, naux)]
    chunks = len(spans)

    def line(x):
        ups, downs = [x], [x]
        for s in range(1, layers):
            up = [(n, n + 1) for n in range(s - 1, layers - 1)]
            down = [(layers - 1 - a, layers - 1 - b) for a, b in up]
            ups.append(lax.ppermute(ups[-1], "col", up))
            downs.append(lax.ppermute(downs[-1], "col", down))
        return ups[:0:-1] + [x] + downs[1:]

    def across(x, d):
        return lax.ppermute(x, "row", [(n, n ^ (2 * d)) for n in range(2 * layers)])

    def swap(x):
        return lax.ppermute(x, "row", [(n, n ^ 1) for n in range(2 * layers)])

    reach = jnp.arange(1 - layers, layers, dtype=jnp.int32) + c
    chips = jnp.bitwise_xor(k, jnp.arange(layers, dtype=jnp.int32))
    sides = jnp.concatenate([chips, jnp.stack([j, 1 - j])]).astype(jnp.int32)
    spots = jnp.where(jnp.logical_and(reach >= 0, reach < layers), reach * piece, -1)
    spots = jnp.concatenate([spots, (k == c).astype(jnp.int32)[None]]).astype(jnp.int32)

    gap_rows = pair_gap(
        lax.dynamic_slice_in_dim(occ_map, c * tile_rows, tile_rows, 0),
        lax.dynamic_slice_in_dim(vir_map, c * tile_rows, tile_rows, 0),
    )[None, :]
    gap_cols = pair_gap(
        lax.dynamic_slice_in_dim(occ_map, row * tile_cols, tile_cols, 0),
        lax.dynamic_slice_in_dim(vir_map, row * tile_cols, tile_cols, 0),
    )[None, :]

    shares = []
    for n, (lo, hi) in enumerate(spans):
        pieces = line(cholesky[:, lo:hi])
        sent = first_product(amplitudes, pieces, spots, sides, layers, strips, False)
        kept = first_product(amplitudes, pieces, spots, sides, layers, strips, True)
        came = swap(sent)

        def rows(d, lo, hi, kept=kept, came=came):
            at = slice(d * piece + lo, d * piece + hi)
            return kept[at] + came[at]

        if layers == 4:
            ends = [0, width, piece] if n == chunks - 1 and strips > 1 else [0, piece]
            done = []
            for lo, hi in zip(ends[:-1], ends[1:]):
                cut = (lo + hi) // 2
                tall = cut - lo
                a0 = jnp.concatenate([rows(1, lo, cut, kept, came), rows(3, lo, cut, kept, came)]).astype(BF)
                b0 = jnp.concatenate([rows(2, cut, hi, kept, came), rows(3, cut, hi, kept, came)]).astype(BF)
                a1, b1 = across(a0, 1), across(b0, 2)
                keep2, came2, a1, b1 = lax.optimization_barrier((kept, came, a1, b1))
                a2 = (rows(2, lo, cut, keep2, came2) + a1[tall:].astype(F32)).astype(BF)
                b2 = (rows(1, cut, hi, keep2, came2) + b1[tall:].astype(F32)).astype(BF)
                a2, b2 = across(a2, 2), across(b2, 1)
                keep2, came2, a1, b1, a2, b2 = lax.optimization_barrier((keep2, came2, a1, b1, a2, b2))
                top = rows(0, lo, cut, keep2, came2) + a1[:tall].astype(F32) + a2.astype(F32)
                low = rows(0, cut, hi, keep2, came2) + b1[:tall].astype(F32) + b2.astype(F32)
                done.append(jnp.concatenate([top, low]).astype(BF))
                kept, came, _, _ = lax.optimization_barrier((kept, came, a0, b0))
        else:
            total = rows(0, 0, piece)
            for d in range(1, layers):
                total = total + across(rows(d, 0, piece).astype(BF), d).astype(F32)
            done = [total.astype(BF)]
        shares.append(jnp.concatenate(done) if len(done) > 1 else done[0])

    splits = [(0, chunks - 1), (chunks - 1, chunks)] if chunks > 1 else [(0, 1)]
    near, far = [], []
    for lo, hi in splits:
        mine = jnp.concatenate(shares[lo:hi], axis=1)
        if layers == 4:
            a, b = across(mine, 1), across(mine, 2)
            parts = [mine, a, b, across(a[:mid], 2), across(b[mid:], 1)]
        else:
            parts = [mine] + [across(mine, d) for d in range(1, layers)]
        near.append(jnp.concatenate(parts, axis=0))
        far.append(swap(near[-1]))

    early = [line(x) for x in shares[:-1]]
    near_at = lambda s: jnp.stack([j, jnp.full_like(j, s)]).astype(jnp.int32)
    far_at = lambda s: jnp.stack([1 - j, jnp.full_like(j, s)]).astype(jnp.int32)

    def strip_of(s):
        if len(done) == 1:
            return done[0][s * width : (s + 1) * width]
        return done[0] if s == 0 else done[1][(s - 1) * width : s * width]

    out = None
    for s in range(strips):
        at = slice(s * width, (s + 1) * width)
        late = line(strip_of(s))
        owners = (chips - c + layers - 1).astype(jnp.int32)
        if layers == 4 and len(early) == 1:
            one, two, own = choose(owners, early[0], late, s * width)
            one, two = across(one, 1), across(two, 2)
            rest, more = one[width:], two[width:]
            rest, more = across(rest, 2), across(more, 1)
            rhs = [(own, 0, 0), (one, 1, 0), (two, 2, 0), (rest, 3, 0), (more, 3, width // 2)]
        else:
            rows = [[x[at] for x in group] for group in early] + [late]
            blocks = [
                jnp.concatenate([lax.select_n(owners[d], *group) for group in rows], axis=1) for d in range(layers)
            ]
            rhs = [(blocks[0], 0, 0)] + [(across(blocks[d], d), d, 0) for d in range(1, layers)]
        shape = (tile_rows, tile_cols)
        out = second_product(near, rhs, gap_rows, gap_cols, near_at(s), sides, strips, layers, out, shape)
        out = second_product(far, rhs, gap_rows, gap_cols, far_at(s), sides, strips, layers, out, shape)
    return out


def solution(mesh):
    layers = mesh.shape["col"]
    assert mesh.shape["row"] == 2 * layers

    def run(*args):
        return body(layers, *args)

    return jax.shard_map(
        run,
        mesh=mesh,
        in_specs=(P("col", "row"), P(("row", "col"), None), P(), P()),
        out_specs=P("col", "row"),
        check_vma=False,
    )
```
